32 devices in a mesh: dp: 4 (over y, x), fsdp: 2 (over core), ctx: 4 (over z).
Axes of the slice: x: 2, y: 2, z: 4, core: 2. Of those that a mesh axis runs over, the one named last changes fastest.
Arguments:
- tokens: bfloat16 [16384, 8192], P(('dp', 'ctx')), may hold values from -6 to 6
- grad_hidden: bfloat16 [16384, 256], P(('dp', 'ctx'), 'fsdp'), may hold values from -0.0625 to 0.0625
- master: float32 [256, 8192], P(('fsdp', 'ctx')), may hold values from -3 to 3
- first_moment: float32 [256, 8192], P(('fsdp', 'ctx')), may hold values from -2 to 2
- second_moment: float32 [256, 8192], P(('fsdp', 'ctx')), may hold values from 0.01 to 1
- clip_scale: float32 [], replicated, may hold values from 0.2 to 1
Outputs:
- new_weights: bfloat16 [256, 8192], P('fsdp')
- new_master: float32 [256, 8192], P(('fsdp', 'ctx'))
- new_first: float32 [256, 8192], P(('fsdp', 'ctx'))
- new_second: float32 [256, 8192], P(('fsdp', 'ctx'))
The draws below stay inside these ranges and needn't reach their ends.
All inputs are finite; a program needn't handle non-finite values.
Results may differ from the reference program's by a relative error of at most 0.005.
Values may be sent and summed in bfloat16 or wider, within the bound.
A program may use at most 128 MiB of HBM per device.

```python
import math
import jax
import jax.numpy as jnp
from jax import lax

D = 8192
TOK_DEV = 1024
STEP = 10
TOKENS = 16384
ROWS = 256
N_DP = 4
N_CTX = 4


def raised(result, key, source, target, parts, factor):
    owner, partner = [(jnp.arange(result.shape[dim]) // (result.shape[dim] // parts)).reshape([-1 if axis == dim else 1 for axis in range(result.ndim)]) for dim in (source, target)]
    chosen = jax.random.permutation(key, parts)[partner]
    strong = (owner == chosen) | (owner == (partner + parts // 2) % parts)
    return jnp.where(strong, factor * result, result)


def block_scale(own_key, extent, shards, least, top_value):
    def one(axis_at, shards_of):
        heights = jax.random.uniform(jax.random.fold_in(jax.random.fold_in(own_key, 6), axis_at), (shards_of,), jnp.float32, least / len(shards), top_value / len(shards))
        return jnp.repeat(jnp.exp(heights), extent[axis_at] // shards_of).reshape((-1,) + (1,) * (len(extent) - axis_at - 1))

    factor_of = one(*shards[0])
    for cut in shards[1:]:
        factor_of = factor_of * one(*cut)
    return factor_of


def normal_values(key, shape, scale, most, cuts=(), kind=jnp.bfloat16):
    drawn = jax.random.normal(key, shape, jnp.float32) * scale
    if len(cuts) > 0:
        drawn = block_scale(key, shape, cuts, -0.22, 0.18) * drawn
    return jnp.clip(drawn, min=-most, max=most).astype(kind)


def gaussian_with(key, dims, scale, most, cuts, heavy, held_as=jnp.bfloat16):
    values = scale * jax.random.normal(key, dims, jnp.float32)
    if cuts:
        values = values * block_scale(key, dims, cuts, -0.22, 0.18)
    return jnp.clip(raised(values, jax.random.fold_in(key, 3), *heavy), -most, most).astype(held_as)


def setup_inputs(seed: int = 0) -> dict:
    key_list = jax.random.split(jax.random.key(seed), 7)
    return {
        "tokens": normal_values(key_list[0], (TOKENS, D), 1.0, 6.0, ((0, 16),)),
        "grad_hidden": gaussian_with(key_list[1], (TOKENS, ROWS), TOKENS ** -0.5, 0.0625, ((0, 16), (1, 2)), (0, 1, 16, 2.0)),
        "master": normal_values(key_list[2], (ROWS, D), 0.5, 3.0, ((0, 8),), jnp.float32),
        "first_moment": normal_values(key_list[3], (ROWS, D), 0.3, 2.0, ((0, 8),), jnp.float32),
        "second_moment": jnp.clip(jnp.exp(math.log(1.0) - 4.6051702 * jax.random.uniform(key_list[4], (ROWS, D), jnp.float32) ** block_scale(key_list[4], (ROWS, D), ((0, 8),), -0.2, 0.2)), 0.01, 1.0),
        "clip_scale": jnp.clip(jax.random.uniform(key_list[5], (), jnp.float32, 0.2, 1.0), 0.2, 1.0),
    }


BETA_ONE = 0.9
BETA_TWO = 0.95
EPSILON = 1e-08
LEARNING_RATE = 0.02
DECAY = 0.1

def adamw(grad_sum, master, first_moment, second_moment, clip_scale):
    scaled = clip_scale * grad_sum
    first_new = BETA_ONE * first_moment + (1.0 - BETA_ONE) * scaled
    second_new = BETA_TWO * second_moment + (1.0 - BETA_TWO) * scaled * scaled
    first_hat = first_new / (1.0 - BETA_ONE ** STEP)
    second_hat = second_new / (1.0 - BETA_TWO ** STEP)
    update = first_hat / (jnp.sqrt(second_hat) + EPSILON)
    fresh_master = master - LEARNING_RATE * (update + DECAY * master)
    return (fresh_master, first_new, second_new)

def reference(tokens, grad_hidden, master, first_moment, second_moment, clip_scale):
    blocks = N_DP * N_CTX
    token_blocks = tokens.reshape(blocks, TOK_DEV, D)
    hidden_blocks = grad_hidden.reshape(blocks, TOK_DEV, ROWS)

    def add_block(total, blocks_pair):
        token_block, hidden_block = blocks_pair
        partial_value = jnp.dot(hidden_block.astype(jnp.float32).T, token_block.astype(jnp.float32), preferred_element_type=jnp.float32)
        partial_value = lax.optimization_barrier(partial_value.astype(jnp.bfloat16)).astype(jnp.float32)
        return (total + partial_value, None)
    grad_sum, _ = lax.scan(add_block, jnp.zeros((ROWS, D), jnp.float32), (token_blocks, hidden_blocks))
    fresh_master, first_new, second_new = adamw(grad_sum, master, first_moment, second_moment, clip_scale)
    return (fresh_master.astype(jnp.bfloat16), fresh_master, first_new, second_new)
```

```python
import functools

import jax
import jax.numpy as jnp
from jax import lax
from jax.experimental import pallas as pl
from jax.experimental.pallas import tpu as pltpu
from jax.sharding import PartitionSpec as P

STEP = 10


BETA_ONE = 0.9
BETA_TWO = 0.95
EPSILON = 1e-08
LEARNING_RATE = 0.02
DECAY = 0.1

CHUNKS = 8
MESH = pl.DeviceIdType.MESH


def adamw(grad_sum, master, first_moment, second_moment, clip_scale):
    scaled = clip_scale * grad_sum
    first_new = BETA_ONE * first_moment + (1.0 - BETA_ONE) * scaled
    second_new = BETA_TWO * second_moment + (1.0 - BETA_TWO) * scaled * scaled
    first_hat = first_new / (1.0 - BETA_ONE**STEP)
    second_hat = second_new / (1.0 - BETA_TWO**STEP)
    update = first_hat / (jnp.sqrt(second_hat) + EPSILON)
    fresh_master = master - LEARNING_RATE * (update + DECAY * master)
    return (fresh_master, first_new, second_new)


def kernel(
    nd, nc, piece, chunks,
    clip_ref, grad_ref, tok_hbm, master_hbm, first_hbm, second_hbm,
    sum_out, weight_out,
    columns, tok, master, first, second,
    part_send, part_recv, mid_send, mid_recv, sum_send, weights,
    tok_sem, state_sem, local_sem,
    part_ss, part_rs, mid_ss, mid_rs, sum_ss, sum_rs, near_ss, near_rs, far_ss, far_rs,
):
    d = lax.axis_index("dp")
    c = lax.axis_index("ctx")
    width = tok.shape[1] // chunks

    def cols(k):
        return pl.ds(pl.multiple_of(k * width, 128), width)

    def tok_copy(k):
        return pltpu.make_async_copy(tok_hbm.at[:, cols(k)], tok.at[:, cols(k)], tok_sem.at[k])

    def state_copies():
        rows = pl.ds(pl.multiple_of(d * piece, piece), piece)
        return [
            pltpu.make_async_copy(src.at[rows], dst, state_sem.at[i])
            for i, (src, dst) in enumerate(
                ((master_hbm, master), (first_hbm, first), (second_hbm, second))
            )
        ]

    def local_copies(k):
        return [
            pltpu.make_async_copy(sum_send.at[k], sum_out.at[d, :, cols(k)], local_sem.at[0, k]),
            pltpu.make_async_copy(weights.at[k], weight_out.at[:, d, :, cols(k)], local_sem.at[1, k]),
        ]

    def send(src, dst, ss, rs, axis, target):
        pltpu.make_async_remote_copy(
            src_ref=src, dst_ref=dst, send_sem=ss, recv_sem=rs,
            device_id={axis: target}, device_id_type=MESH,
        ).start()

    def take(like, sem):
        pltpu.make_async_copy(like, like, sem).wait()

    @pl.loop(0, chunks)
    def _(k):
        tok_copy(k).start()

    for copy in state_copies():
        copy.start()

    barrier = pltpu.get_barrier_semaphore()
    for j in range(1, nd):
        pl.semaphore_signal(
            barrier, inc=1, device_id={"dp": lax.rem(d + j, nd)}, device_id_type=MESH
        )
    for j in range(1, nc):
        pl.semaphore_signal(
            barrier, inc=1, device_id={"ctx": lax.rem(c + j, nc)}, device_id_type=MESH
        )
    columns[...] = grad_ref[...].T
    pl.semaphore_wait(barrier, nd + nc - 2)

    @pl.loop(0, chunks)
    def _(k):
        tok_copy(k).wait()
        partial = jnp.dot(columns[...], tok[:, cols(k)], preferred_element_type=jnp.float32)
        partial = partial.reshape(nc, nd, piece, width)
        for e in range(nd):
            part_send[k, e] = partial[:, e].astype(jnp.bfloat16)
        for j in range(1, nd):
            to = lax.rem(d + j, nd)
            send(
                part_send.at[k, to], part_recv.at[k, j - 1], part_ss.at[k], part_rs.at[k], "dp", to
            )

    for copy in state_copies():
        copy.wait()

    @pl.loop(0, chunks + 2)
    def _(t):
        @pl.when(t < chunks)
        def _():
            k = t
            take(part_recv.at[k], part_rs.at[k])
            total = part_send[k, d].astype(jnp.float32)
            for j in range(nd - 1):
                total = total + part_recv[k, j].astype(jnp.float32)
            mid_send[k] = total.astype(jnp.bfloat16)
            for j in range(1, nc):
                to = lax.rem(c + j, nc)
                send(
                    mid_send.at[k, to], mid_recv.at[k, j - 1], mid_ss.at[k], mid_rs.at[k], "ctx", to
                )

        @pl.when(jnp.logical_and(t >= 1, t < chunks + 1))
        def _():
            k = t - 1
            take(mid_recv.at[k], mid_rs.at[k])
            total = mid_send[k, c].astype(jnp.float32)
            for j in range(nc - 1):
                total = total + mid_recv[k, j].astype(jnp.float32)
            rounded = total.astype(jnp.bfloat16)
            sum_send[k] = rounded
            fresh, _, _ = adamw(
                rounded.astype(jnp.float32),
                master[:, cols(k)], first[:, cols(k)], second[:, cols(k)], clip_ref[0],
            )
            weights[k, c] = fresh.astype(jnp.bfloat16)
            for j in range(1, nc):
                send(
                    weights.at[k, c], weights.at[k, c], near_ss.at[k], near_rs.at[k],
                    "ctx", lax.rem(c + j, nc),
                )
            for j in range(1, nd):
                send(
                    sum_send.at[k], sum_out.at[d, :, cols(k)], sum_ss.at[k], sum_rs.at[k],
                    "dp", lax.rem(d + j, nd),
                )

        @pl.when(t >= 2)
        def _():
            k = t - 2
            take(mid_recv.at[k], near_rs.at[k])
            for j in range(1, nd):
                send(
                    weights.at[k], weight_out.at[:, d, :, cols(k)], far_ss.at[k], far_rs.at[k],
                    "dp", lax.rem(d + j, nd),
                )
            for copy in local_copies(k):
                copy.start()

    @pl.loop(0, chunks)
    def _(k):
        for copy in local_copies(k):
            copy.wait()
        take(part_recv.at[k], part_ss.at[k])
        take(mid_recv.at[k], mid_ss.at[k])
        take(mid_recv.at[k], near_ss.at[k])
        take(part_recv.at[k, :, 0], sum_ss.at[k])
        take(part_recv.at[k, :, 0], sum_rs.at[k])
        take(part_recv.at[k], far_ss.at[k])
        take(part_recv.at[k], far_rs.at[k])


def per_device(tokens, grad_hidden, master, first_moment, second_moment, clip_scale):
    nc = lax.axis_size("ctx")
    nd = lax.axis_size("dp")
    row_dev, dim = master.shape
    piece = row_dev // nd
    tok_rows, rows = grad_hidden.shape
    width = dim // CHUNKS
    bf16, f32 = jnp.bfloat16, jnp.float32
    dma = pltpu.SemaphoreType.DMA
    hbm = pl.BlockSpec(memory_space=pl.ANY)
    grad_sum, weights = pl.pallas_call(
        functools.partial(kernel, nd, nc, piece, CHUNKS),
        out_shape=(
            jax.ShapeDtypeStruct((nd, piece, dim), bf16),
            jax.ShapeDtypeStruct((nc, nd, piece, dim), bf16),
        ),
        in_specs=[
            pl.BlockSpec(memory_space=pltpu.SMEM),
            pl.BlockSpec(memory_space=pltpu.VMEM),
            hbm, hbm, hbm, hbm,
        ],
        out_specs=(hbm, hbm),
        scratch_shapes=[
            pltpu.VMEM((rows, tok_rows), bf16),
            pltpu.VMEM((tok_rows, dim), bf16),
            pltpu.VMEM((piece, dim), f32),
            pltpu.VMEM((piece, dim), f32),
            pltpu.VMEM((piece, dim), f32),
            pltpu.VMEM((CHUNKS, nd, nc, piece, width), bf16),
            pltpu.VMEM((CHUNKS, nd - 1, nc, piece, width), bf16),
            pltpu.VMEM((CHUNKS, nc, piece, width), bf16),
            pltpu.VMEM((CHUNKS, nc - 1, piece, width), bf16),
            pltpu.VMEM((CHUNKS, piece, width), bf16),
            pltpu.VMEM((CHUNKS, nc, piece, width), bf16),
            dma((CHUNKS,)), dma((3,)), dma((2, CHUNKS)),
        ] + [dma((CHUNKS,))] * 10,
        compiler_params=pltpu.CompilerParams(
            collective_id=0, has_side_effects=True, vmem_limit_bytes=56 << 20
        ),
        cost_estimate=pl.CostEstimate(
            flops=2 * rows * tok_rows * dim,
            bytes_accessed=2 * tok_rows * dim + 4 * rows * dim,
            transcendentals=0,
        ),
    )(clip_scale.reshape(1), grad_hidden, tokens, master, first_moment, second_moment)
    new_master, new_first, new_second = adamw(
        grad_sum.reshape(row_dev, dim).astype(f32), master, first_moment, second_moment, clip_scale
    )
    return (weights.reshape(rows, dim), new_master, new_first, new_second)


def solution(mesh):
    in_specs = (
        P(("dp", "ctx"), None),
        P(("dp", "ctx"), "fsdp"),
        P(("fsdp", "ctx"), None),
        P(("fsdp", "ctx"), None),
        P(("fsdp", "ctx"), None),
        P(),
    )
    out_specs = (
        P("fsdp", None),
        P(("fsdp", "ctx"), None),
        P(("fsdp", "ctx"), None),
        P(("fsdp", "ctx"), None),
    )
    return jax.shard_map(
        per_device, mesh=mesh, in_specs=in_specs, out_specs=out_specs, check_vma=False
    )
```
